32 devices in a mesh: seq: 4 (over x, core), fsdp: 8 (over z, y).
Axes of the slice: x: 2, y: 2, z: 4, core: 2. Of those that a mesh axis runs over, the one named last changes fastest.
Arguments:
- tokens: bfloat16 [8, 1024, 1024], P('fsdp', 'seq'), may hold values from -6 to 6
- doc_lengths: int32 [8, 8], P('fsdp'), may hold values from 1 to 512, 1024 in all within a row
- ln1_gain: bfloat16 [1024], P('fsdp'), may hold values from 0.5 to 1.5
- ln1_bias: bfloat16 [1024], P('fsdp'), may hold values from -1.25 to 1.25
- ln2_gain: bfloat16 [1024], P('fsdp'), may hold values from 0.5 to 1.5
- ln2_bias: bfloat16 [1024], P('fsdp'), may hold values from -1.25 to 1.25
- qkv_weight: bfloat16 [1024, 3072], P('fsdp'), may hold values from -0.25 to 0.25
- qkv_bias: bfloat16 [3072], P('fsdp'), may hold values from -1.25 to 1.25
- dense_weight: bfloat16 [1024, 1024], P('fsdp'), may hold values from -1.5 to 1.5
- dense_bias: bfloat16 [1024], P('fsdp'), may hold values from -1.25 to 1.25
- up_weight: bfloat16 [1024, 4096], P('fsdp'), may hold values from -0.1875 to 0.1875
- up_bias: bfloat16 [4096], P('fsdp'), may hold values from -1.25 to 1.25
- down_weight: bfloat16 [4096, 1024], P('fsdp'), may hold values from -0.09375 to 0.09375
- down_bias: bfloat16 [1024], P('fsdp'), may hold values from -1.25 to 1.25
- cotangent: bfloat16 [8, 1024, 1024], P('fsdp', 'seq'), may hold values from -6 to 6
Outputs:
- mixed: bfloat16 [8, 1024, 1024], P('fsdp', 'seq')
- tokens_grad: float32 [8, 1024, 1024], P('fsdp', 'seq')
- ln1_gain_grad: float32 [1024], P('fsdp')
- ln1_bias_grad: float32 [1024], P('fsdp')
- ln2_gain_grad: float32 [1024], P('fsdp')
- ln2_bias_grad: float32 [1024], P('fsdp')
- qkv_weight_grad: float32 [1024, 3072], P('fsdp')
- qkv_bias_grad: float32 [3072], P('fsdp')
- dense_weight_grad: float32 [1024, 1024], P('fsdp')
- dense_bias_grad: float32 [1024], P('fsdp')
- up_weight_grad: float32 [1024, 4096], P('fsdp')
- up_bias_grad: float32 [4096], P('fsdp')
- down_weight_grad: float32 [4096, 1024], P('fsdp')
- down_bias_grad: float32 [1024], P('fsdp')
The draws below stay inside these ranges and needn't reach their ends.
Inputs may be any that keep to these rules, and one draw needn't show every extreme that they name: `doc_lengths`: each row holds the lengths of the 8 documents of one pack in order; they sum to 1024 and the longest is exactly 512.
All inputs are finite; a program needn't handle non-finite values.
Results may differ from the reference program's by a relative error of at most 0.017.
Values may be sent and summed in bfloat16 or wider, within the bound.
No kernel may reach another device: no remote copies, remote signals or barrier semaphores. Data moves between devices by JAX's collectives and lax.ppermute only.
A program may use at most 192 MiB of HBM per device.

```python
import math
import jax
import jax.numpy as jnp
import numpy as np
from jax import lax

D = 1024
HEADS = 16
HEAD_DIM = 64
ROT = 16
FF = 4096
DOCS = 8
PACK_TOK = 1024
PACKS = 8
DOC_MOST = 512


def level_of(stream_key, extent, cuts, smallest, largest):
    level = 1.0
    for dim, parts in cuts:
        draws = jax.random.uniform(jax.random.fold_in(jax.random.fold_in(stream_key, 6), dim), (parts,), jnp.float32, smallest / len(cuts), largest / len(cuts))
        level = level * jnp.repeat(jnp.exp(draws), extent[dim] // parts).reshape((-1,) + (1,) * (len(extent) - 1 - dim))
    return level


def profile(number_of, total, reach, slope):
    portions = [(1 << 20) // math.isqrt(standing ** slope) + 1 for standing in range(2, number_of + 1)]
    rest, given = total - reach - (number_of - 1), [1] * (number_of - 1)
    while rest > 0:
        candidates = [i for i in range(number_of - 1) if given[i] < reach]
        mass, remaining = sum([portions[i] for i in candidates]), rest
        for i in candidates:
            extra = min(reach - given[i], max(1, remaining * portions[i] // mass), rest)
            given[i] = given[i] + extra
            rest = rest - extra
    return np.array([reach] + given)


def ragged(own_key, count, total, bound, skew):
    if count == 2:
        one = jax.random.randint(own_key, (), max(1, total - bound), min(bound, total - 1) + 1)
        return jnp.stack([one, total - one])
    tallies = jnp.asarray(profile(count, total, bound, skew), jnp.int32)
    twos = (count - 1) // 2
    source_of, taker = tallies[1:1 + 2 * twos:2], tallies[2:2 + 2 * twos:2]
    room = jnp.minimum(source_of - 1, bound - taker)
    passed = jax.random.randint(jax.random.fold_in(own_key, 1), (twos,), 0, 1 << 20) % (room + 1)
    tallies = tallies.at[1:1 + 2 * twos:2].set(source_of - passed).at[2:2 + 2 * twos:2].set(taker + passed)
    return tallies[jax.random.permutation(jax.random.fold_in(own_key, 2), count)]


def bell_draw(rng, extent, scale, most, shards=(), held_as=jnp.bfloat16):
    loudness = level_of(rng, extent, shards, -0.22, 0.18) if shards else 1.0
    values = jax.random.normal(rng, extent, jnp.float32) * scale * loudness
    return jnp.minimum(jnp.maximum(values, -most), most).astype(held_as)


def setup_inputs(seed: int = 0) -> dict:
    seeds = jax.random.split(jax.random.key(seed), 16)
    return {
        "tokens": bell_draw(seeds[0], (PACKS, PACK_TOK, D), 1.0, 6.0, ((0, 8), (1, 4))),
        "doc_lengths": jax.vmap(lambda own: ragged(own, DOCS, PACK_TOK, DOC_MOST, 2))(jax.random.split(seeds[1], PACKS)).reshape((PACKS, DOCS)).astype(jnp.int32),
        "ln1_gain": jnp.clip(1.0 + 0.1 * jax.random.normal(seeds[2], (D,), jnp.float32), 0.5, 1.5).astype(jnp.bfloat16),
        "ln1_bias": bell_draw(seeds[3], (D,), 0.2, 1.25, ((0, 8),)),
        "ln2_gain": jnp.clip(1.0 + 0.1 * jax.random.normal(seeds[4], (D,), jnp.float32), 0.5, 1.5).astype(jnp.bfloat16),
        "ln2_bias": bell_draw(seeds[5], (D,), 0.2, 1.25, ((0, 8),)),
        "qkv_weight": bell_draw(seeds[6], (D, 3 * D), (D // 2) ** -0.5, 0.25, ((0, 8),)),
        "qkv_bias": bell_draw(seeds[7], (3 * D,), 0.2, 1.25, ((0, 8),)),
        "dense_weight": bell_draw(seeds[8], (D, D), (D // 64) ** -0.5, 1.5, ((0, 8),)),
        "dense_bias": bell_draw(seeds[9], (D,), 0.2, 1.25, ((0, 8),)),
        "up_weight": bell_draw(seeds[10], (D, FF), D ** -0.5, 0.1875, ((0, 8),)),
        "up_bias": bell_draw(seeds[11], (FF,), 0.2, 1.25, ((0, 8),)),
        "down_weight": bell_draw(seeds[12], (FF, D), FF ** -0.5, 0.09375, ((0, 8),)),
        "down_bias": bell_draw(seeds[13], (D,), 0.2, 1.25, ((0, 8),)),
        "cotangent": bell_draw(seeds[14], (PACKS, PACK_TOK, D), 1.0, 6.0, ((0, 8), (1, 4))),
    }


@jax.custom_vjp
def low(v):
    return lax.optimization_barrier(v.astype(jnp.bfloat16)).astype(jnp.float32)

@jax.custom_vjp
def low_back(v):
    return v

def low_keep(v):
    return (low(v), None)

def low_pass(kept, grad):
    return (grad,)

def back_keep(v):
    return (v, None)

def back_low(kept, grad):
    return (low(grad),)
low.defvjp(low_keep, low_pass)
low_back.defvjp(back_keep, back_low)
EPSILON = 1e-05
SCORE_SCALE = 0.125
MASKED_SCORE = -1e+30
HIGHEST = lax.Precision.HIGHEST

def layer_norm(values, gain_vec, shift_vec):
    row_mean = lax.optimization_barrier(jnp.mean(values, axis=-1, keepdims=True))
    centered = values - row_mean
    spread = lax.optimization_barrier(jnp.mean(centered * centered, axis=-1, keepdims=True))
    return centered * lax.rsqrt(spread + EPSILON) * gain_vec + shift_vec

def rotary_tables(position):
    freqs = 1.0 / 10000.0 ** (jnp.arange(0, ROT, 2, dtype=jnp.float32) / ROT)
    angles = position.astype(jnp.float32)[:, None] * freqs[None, :]
    angles = jnp.concatenate([angles, angles], axis=-1)
    return (jnp.cos(angles)[:, None, None, :], jnp.sin(angles)[:, None, None, :])

def rotate_qkv(flat_rows, cosine, sine_table):
    shaped = flat_rows.reshape(flat_rows.shape[0], HEADS, 3, HEAD_DIM)
    half_rot = ROT // 2
    leading = shaped[..., :ROT]
    turned = jnp.concatenate([-leading[..., half_rot:], leading[..., :half_rot]], axis=-1)
    rotated = leading * cosine + turned * sine_table
    chosen = (jnp.arange(3) < 2)[None, None, :, None]
    rotated = jnp.where(chosen, rotated, leading)
    return jnp.concatenate([rotated, shaped[..., ROT:]], axis=-1).reshape(flat_rows.shape)

def doc_layout(lengths, row_count):
    doc_ends = jnp.cumsum(lengths).astype(jnp.int32)
    doc_starts = doc_ends - lengths
    places = jnp.arange(row_count, dtype=jnp.int32)
    segment = lax.optimization_barrier(jnp.sum((places[:, None] >= doc_ends[None, :]).astype(jnp.int32), axis=1))
    begins = lax.optimization_barrier(jnp.max(jnp.where(doc_starts[None, :] <= places[:, None], doc_starts[None, :], 0), axis=1))
    return (segment, places - begins)

def head_attention(queries, key_rows, value_rows, segment, block_rows, window):
    row_count = queries.shape[0]
    zero_rows = jnp.zeros((window, queries.shape[1]), queries.dtype)
    key_pad = jnp.concatenate([zero_rows, key_rows], axis=0)
    value_pad = jnp.concatenate([zero_rows, value_rows], axis=0)
    segment_pad = jnp.concatenate([jnp.full((window,), -1, jnp.int32), segment])
    span_rows = window + block_rows

    def one_block(start):
        query_blk = lax.dynamic_slice_in_dim(queries, start, block_rows, 0)
        key_blk = lax.dynamic_slice_in_dim(key_pad, start, span_rows, 0)
        value_blk = lax.dynamic_slice_in_dim(value_pad, start, span_rows, 0)
        seg_query = lax.dynamic_slice_in_dim(segment, start, block_rows, 0)
        seg_key = lax.dynamic_slice_in_dim(segment_pad, start, span_rows, 0)
        scores = low_back(jnp.dot(query_blk, key_blk.T, precision=HIGHEST) * SCORE_SCALE)
        row_index = jnp.arange(block_rows)[:, None]
        col_index = jnp.arange(span_rows)[None, :]
        allowed = (seg_query[:, None] == seg_key[None, :]) & (col_index <= row_index + window)
        scores = jnp.where(allowed, scores, MASKED_SCORE)
        row_max = lax.optimization_barrier(jnp.max(scores, axis=-1, keepdims=True))
        weights = jnp.exp(scores - row_max)
        row_sum = lax.optimization_barrier(jnp.sum(weights, axis=-1, keepdims=True))
        prob_low = low(weights / row_sum)
        return jnp.dot(prob_low, value_blk, precision=HIGHEST)
    starts = jnp.arange(row_count // block_rows, dtype=jnp.int32) * block_rows
    out_blocks = lax.map(jax.checkpoint(one_block), starts)
    return out_blocks.reshape(row_count, HEAD_DIM)

def pack_forward(inputs, lengths, params):
    gain_one, shift_one, gain_two, shift_two, qkv_w, qkv_b, dense_w, dense_b, up_w, up_b, down_w, down_b = params
    row_count = inputs.shape[0]
    block_rows = min(512, row_count)
    window = row_count // 2
    segment, position = doc_layout(lengths, row_count)
    cosine, sine_table = rotary_tables(position)
    normed_one = low(layer_norm(inputs, gain_one, shift_one))
    normed_two = low(layer_norm(inputs, gain_two, shift_two))
    projected = low_back(jnp.dot(normed_one, qkv_w, precision=HIGHEST) + qkv_b)
    turned = low(low_back(rotate_qkv(projected, cosine, sine_table)))
    shaped = turned.reshape(row_count, HEADS, 3, HEAD_DIM).transpose(1, 2, 0, 3)

    def per_head(head_trio):
        return head_attention(head_trio[0], head_trio[1], head_trio[2], segment, block_rows, window)
    mixed_heads = lax.map(per_head, shaped)
    attended = low(low_back(mixed_heads.transpose(1, 0, 2).reshape(row_count, D)))
    dense_out = jnp.dot(attended, dense_w, precision=HIGHEST) + dense_b
    pre_act = low_back(jnp.dot(normed_two, up_w, precision=HIGHEST) + up_b)
    hidden = low(jax.nn.gelu(pre_act, approximate=False))
    feed_out = jnp.dot(hidden, down_w, precision=HIGHEST) + down_b
    return inputs + dense_out + feed_out

def reference(tokens, doc_lengths, ln1_gain, ln1_bias, ln2_gain, ln2_bias, qkv_weight, qkv_bias, dense_weight, dense_bias, up_weight, up_bias, down_weight, down_bias, cotangent):
    weights = (ln1_gain.astype(jnp.float32), ln1_bias.astype(jnp.float32), ln2_gain.astype(jnp.float32), ln2_bias.astype(jnp.float32), qkv_weight.astype(jnp.float32), qkv_bias.astype(jnp.float32), dense_weight.astype(jnp.float32), dense_bias.astype(jnp.float32), up_weight.astype(jnp.float32), up_bias.astype(jnp.float32), down_weight.astype(jnp.float32), down_bias.astype(jnp.float32))
    saved_pack = jax.checkpoint(pack_forward)

    def forward(inputs_all, params):

        def one_pack(pair):
            return saved_pack(pair[0], pair[1], params)
        return lax.map(one_pack, (inputs_all, doc_lengths))
    result, pull_back = jax.vjp(forward, tokens.astype(jnp.float32), weights)
    grad_inputs, grad_params = pull_back(cotangent.astype(jnp.float32))
    return (result.astype(jnp.bfloat16), grad_inputs, grad_params[0], grad_params[1], grad_params[2], grad_params[3], grad_params[4], grad_params[5], grad_params[6], grad_params[7], grad_params[8], grad_params[9], grad_params[10], grad_params[11])
```

```python
import functools

import jax
import jax.numpy as jnp
from jax import lax
from jax.experimental import pallas as pl
from jax.experimental.pallas import tpu as pltpu
from jax.sharding import PartitionSpec as P

HEAD_DIM = 64
ROT = 16
EPSILON = 1e-05
SCORE_SCALE = 0.125
MASKED_SCORE = -1e30
BF16 = jnp.bfloat16
F32 = jnp.float32
CONTRACT_ROWS = (((1,), (1,)), ((), ()))
CONTRACT_COLS = (((0,), (0,)), ((), ()))


def dot(a, b):
    return jnp.dot(a, b, preferred_element_type=F32)


def dot_nt(a, b):
    return lax.dot_general(a, b, CONTRACT_ROWS, preferred_element_type=F32)


def dot_tn(a, b):
    return lax.dot_general(a, b, CONTRACT_COLS, preferred_element_type=F32)


class Ring:
    def __init__(self, axis, size):
        self.axis, self.size = axis, size
        self.cycle = [i for i in range(0, size, 2)] + [i for i in range(size - 1, 0, -2)]
        self.up = [(self.cycle[i], self.cycle[(i + 1) % size]) for i in range(size)]
        self.down = [(b, a) for a, b in self.up]
        me = lax.axis_index(axis)
        self.me = me
        self.place = jnp.where(me % 2 == 0, me // 2, size - 1 - me // 2)

    def at(self, offset):
        place = lax.rem(self.place + (offset + self.size), self.size)
        half = self.size // 2
        return jnp.where(place < half, 2 * place, 2 * (self.size - 1 - place) + 1)

    def gather(self, chunk, longer_up):
        ups = self.size // 2 if longer_up else self.size - 1 - self.size // 2
        downs = self.size - 1 - ups
        found = [(self.me, chunk)]
        rising, falling = chunk, chunk
        for step in range(1, max(ups, downs) + 1):
            if step <= ups:
                rising = lax.ppermute(rising, self.axis, self.up)
                found.append((self.at(-step), rising))
            if step <= downs:
                falling = lax.ppermute(falling, self.axis, self.down)
                found.append((self.at(step), falling))
        return found

    def scatter_sum(self, chunk_of, longer_up):
        ups = self.size // 2 if longer_up else self.size - 1 - self.size // 2
        downs = self.size - 1 - ups
        rising = falling = None
        for step in range(max(ups, downs), 0, -1):
            if step <= ups:
                own = chunk_of(self.at(step))
                total = own if rising is None else own + rising.astype(F32)
                rising = lax.ppermute(total.astype(BF16), self.axis, self.up)
            if step <= downs:
                own = chunk_of(self.at(-step))
                total = own if falling is None else own + falling.astype(F32)
                falling = lax.ppermute(total.astype(BF16), self.axis, self.down)
        return chunk_of(self.me) + rising.astype(F32) + falling.astype(F32)


class Cube:
    def __init__(self, axis, size):
        self.axis, self.size = axis, size
        self.me = lax.axis_index(axis)
        self.bits = [1 << i for i in range(size.bit_length() - 1)]

    def swap(self, value, mask):
        return lax.ppermute(value, self.axis, [(i, i ^ mask) for i in range(self.size)])

    def gather(self, value):
        found = {0: value}
        for bit in reversed(self.bits):
            for mask in list(found):
                found[mask | bit] = self.swap(found[mask], bit)
        return found

    def gather_rows(self, value):
        found = self.gather(value)
        rows = value.shape[0]
        whole = jnp.zeros((self.size * rows,) + value.shape[1:], value.dtype)
        for mask, part in found.items():
            whole = lax.dynamic_update_slice_in_dim(whole, part, (self.me ^ mask) * rows, 0)
        return whole

    def scatter_sum(self, partial):
        rows = partial.shape[0] // self.size

        def block(mask):
            return lax.dynamic_slice_in_dim(partial, (self.me ^ mask) * rows, rows, 0)

        kept = {mask: block(mask) for mask in range(self.size)}
        for bit in self.bits:
            received = {
                mask ^ bit: self.swap(kept[mask].astype(BF16), bit) for mask in kept if mask & bit
            }
            kept = {
                mask: kept[mask] + received[mask].astype(F32) for mask in kept if not mask & bit
            }
        return kept[0]

    def total(self, value):
        for bit in self.bits:
            value = value + self.swap(value, bit)
        return value

    def exchange(self, piece_for):
        found = {0: piece_for(self.me)}
        for mask in range(1, self.size):
            found[mask] = self.swap(piece_for(self.me ^ mask), mask)
        return found


def join_rows(parts):
    rows = parts[0][1].shape[0]
    whole = jnp.zeros((len(parts) * rows,) + parts[0][1].shape[1:], parts[0][1].dtype)
    for index, part in parts:
        whole = lax.dynamic_update_slice_in_dim(whole, part, index * rows, 0)
    return whole


def turn(values, cosine, sine_low, sine_high):
    width = values.shape[1]
    half = ROT // 2
    return (
        values * cosine
        + pltpu.roll(values, width - half, 1) * sine_low
        + pltpu.roll(values, half, 1) * sine_high
    )


def attention_body(
    heads, block_rows, window,
    normed, weight, bias, grad_out, cosine, sine_low, sine_high, first,
    out, grad_z,
    query_s, key_s, value_s, grad_s, grad_query, grad_key, grad_value, out_s,
):
    rows = normed.shape[0]
    pair = 2 * HEAD_DIM
    trio = 3 * HEAD_DIM
    chunk = block_rows

    def project(step, carry):
        here = pl.ds(pl.multiple_of(step * chunk, chunk), chunk)
        z = dot(normed[here, :], weight[...]) + bias[...]
        cos, low, high = cosine[here, :], sine_low[here, :], sine_high[here, :]
        for head in range(heads):
            base = head * trio
            turned = turn(z[:, base : base + pair], cos, low, high)
            query_s[head, here, :] = (turned[:, :HEAD_DIM].astype(BF16).astype(F32) * SCORE_SCALE).astype(BF16)
            key_s[head, here, :] = turned[:, HEAD_DIM:].astype(BF16)
            value_s[head, here, :] = z[:, base + pair : base + trio].astype(BF16)
            grad_s[head, here, :] = grad_out[here, head * HEAD_DIM : (head + 1) * HEAD_DIM]
        return carry

    lax.fori_loop(0, rows // chunk, project, 0)
    grad_key[...] = jnp.zeros_like(grad_key)
    grad_value[...] = jnp.zeros_like(grad_value)

    def one_head(head, carry):
        for step in range(rows // block_rows):
            q0 = step * block_rows
            k0 = max(0, q0 - window)
            k1 = q0 + block_rows
            q = query_s[head, q0:k1, :]
            do = grad_s[head, q0:k1, :]
            k = key_s[head, k0:k1, :]
            v = value_s[head, k0:k1, :]
            row = q0 + lax.broadcasted_iota(jnp.int32, (block_rows, k1 - k0), 0)
            col = k0 + lax.broadcasted_iota(jnp.int32, (block_rows, k1 - k0), 1)
            allowed = (col <= row) & (col >= first[q0:k1, :])
            scores = jnp.where(allowed, dot_nt(q, k), MASKED_SCORE)
            top = jnp.max(scores, axis=1, keepdims=True)
            weights = jnp.exp(scores - top)
            weights = weights / jnp.sum(weights, axis=1, keepdims=True)
            low = weights.astype(BF16)
            out_s[head, q0:k1, :] = dot(low, v).astype(BF16)
            grad_p = dot_nt(do, v)
            inner = jnp.sum(weights * grad_p, axis=1, keepdims=True)
            grad_sc = (weights * (grad_p - inner)).astype(BF16)
            grad_query[head, q0:k1, :] = dot(grad_sc, k) * SCORE_SCALE
            grad_key[head, k0:k1, :] += dot_tn(grad_sc, q)
            grad_value[head, k0:k1, :] += dot_tn(low, do)
        return carry

    lax.fori_loop(0, heads, one_head, 0)

    def finish(step, carry):
        here = pl.ds(pl.multiple_of(step * chunk, chunk), chunk)
        cos, low, high = cosine[here, :], sine_low[here, :], sine_high[here, :]
        for head in range(heads):
            base = head * trio
            both = jnp.concatenate([grad_query[head, here, :], grad_key[head, here, :]], axis=1)
            grad_z[here, base : base + pair] = turn(both, cos, -low, -high).astype(BF16)
            grad_z[here, base + pair : base + trio] = grad_value[head, here, :].astype(BF16)
            out[here, head * HEAD_DIM : (head + 1) * HEAD_DIM] = out_s[head, here, :]
        return carry

    lax.fori_loop(0, rows // chunk, finish, 0)


def attention(normed, weight, bias, grad_out, tables, first):
    rows = normed.shape[0]
    heads = weight.shape[1] // (3 * HEAD_DIM)
    block_rows = min(256, rows)
    window = rows // 2
    per_head = (heads, rows, HEAD_DIM)
    return pl.pallas_call(
        functools.partial(attention_body, heads, block_rows, window),
        out_shape=(
            jax.ShapeDtypeStruct((rows, heads * HEAD_DIM), BF16),
            jax.ShapeDtypeStruct((rows, heads * 3 * HEAD_DIM), BF16),
        ),
        scratch_shapes=[pltpu.VMEM(per_head, BF16) for _ in range(4)]
        + [pltpu.VMEM(per_head, F32) for _ in range(3)]
        + [pltpu.VMEM(per_head, BF16)],
        compiler_params=pltpu.CompilerParams(vmem_limit_bytes=56 * 1024 * 1024),
        name="attention",
    )(normed, weight, bias, grad_out, *tables, first)


def doc_layout(lengths, row_count):
    doc_ends = jnp.cumsum(lengths)
    doc_starts = doc_ends - lengths
    places = jnp.arange(row_count, dtype=jnp.int32)
    return jnp.max(
        jnp.where(doc_starts[None, :] <= places[:, None], doc_starts[None, :], 0), axis=1
    )


def rotary_tables(position):
    freqs = 1.0 / 10000.0 ** (jnp.arange(0, ROT, 2, dtype=F32) / ROT)
    angles = position.astype(F32)[:, None] * freqs[None, :]
    cos, sin = jnp.cos(angles), jnp.sin(angles)
    rows, half = position.shape[0], ROT // 2
    ones = jnp.ones((rows, HEAD_DIM - ROT), F32)
    zeros = jnp.zeros((rows, HEAD_DIM - ROT), F32)
    gap = jnp.zeros((rows, half), F32)
    cosine = jnp.concatenate([cos, cos, ones], axis=1)
    low = jnp.concatenate([-sin, gap, zeros], axis=1)
    high = jnp.concatenate([gap, sin, zeros], axis=1)
    return tuple(jnp.concatenate([t, t], axis=1) for t in (cosine, low, high))


def gelu_and_slope(values):
    upper = 0.5 * (1.0 + lax.erf(values * (0.5**0.5)))
    bell = jnp.exp(-0.5 * values * values) * 0.3989422804014327
    return values * upper, upper + values * bell


def per_device(
    tokens, doc_lengths, ln1_gain, ln1_bias, ln2_gain, ln2_bias,
    qkv_weight, qkv_bias, dense_weight, dense_bias,
    up_weight, up_bias, down_weight, down_bias, cotangent,
):
    seq, fsdp = lax.axis_size("seq"), lax.axis_size("fsdp")
    cube, ring = Cube("seq", seq), Ring("fsdp", fsdp)
    me = cube.me
    local_rows, width = tokens.shape[1], tokens.shape[2]
    row_count = local_rows * seq
    shard = width // fsdp
    hidden_all = up_weight.shape[1]
    unit = hidden_all // fsdp // seq
    qkv_cols = qkv_weight.shape[1] // seq
    dense_unit = shard // seq
    spans = fsdp // seq

    x_own, g_own = tokens[0], cotangent[0]

    small = jnp.concatenate(
        [ln1_gain, ln1_bias, ln2_gain, ln2_bias, dense_bias, down_bias, qkv_bias, up_bias]
    )[None]
    up_piece = lax.dynamic_slice_in_dim(
        up_weight.reshape(shard, fsdp, seq, unit), me, 1, 2
    ).reshape(shard, fsdp * unit)
    down_piece = lax.dynamic_slice_in_dim(down_weight, me * unit, unit, 0)
    qkv_piece = lax.dynamic_slice_in_dim(qkv_weight, me * qkv_cols, qkv_cols, 1)
    dense_piece = lax.dynamic_slice_in_dim(dense_weight, me * dense_unit, dense_unit, 0)

    x_all = cube.gather_rows(x_own)
    small_all = join_rows(ring.gather(small, True))
    dense_cross = join_rows(ring.gather(dense_piece, False)).reshape(fsdp, dense_unit, width)
    qkv_w = join_rows(ring.gather(qkv_piece, True))
    g_all = cube.gather_rows(g_own)
    up_w = join_rows(ring.gather(up_piece, True))
    down_w = join_rows(ring.gather(down_piece, False))

    pieces = cube.exchange(
        lambda other: lax.dynamic_slice_in_dim(dense_cross, other * spans, spans, 0)
    )
    dense_w = jnp.zeros((spans, seq, dense_unit, width), BF16)
    for mask, piece in pieces.items():
        dense_w = lax.dynamic_update_slice_in_dim(dense_w, piece[:, None], me ^ mask, 1)
    dense_w = dense_w.reshape(spans * shard, width)

    def vector(index):
        return small_all[:, index * shard : (index + 1) * shard].reshape(width).astype(F32)

    gain_one, shift_one, gain_two, shift_two, dense_b, down_b = (vector(i) for i in range(6))
    base = 6 * shard
    qkv_b = small_all[:, base : base + qkv_bias.shape[0]].reshape(seq, qkv_cols)
    qkv_b = lax.dynamic_slice_in_dim(qkv_b, me, 1, 0).astype(F32)
    up_b = small_all[:, base + qkv_bias.shape[0] :].reshape(fsdp, seq, unit)
    up_b = lax.dynamic_slice_in_dim(up_b, me, 1, 1).reshape(1, fsdp * unit).astype(F32)

    begins = doc_layout(doc_lengths[0], row_count)
    tables = rotary_tables(jnp.arange(row_count, dtype=jnp.int32) - begins)

    xf = x_all.astype(F32)
    mean = jnp.mean(xf, axis=-1, keepdims=True)
    centered = xf - mean
    scale = lax.rsqrt(jnp.mean(centered * centered, axis=-1, keepdims=True) + EPSILON)
    xhat = centered * scale
    normed_one = (xhat * gain_one + shift_one).astype(BF16)
    normed_two = (xhat * gain_two + shift_two).astype(BF16)

    grad_att = dot_nt(g_all, dense_w).astype(BF16)
    attended, grad_z = attention(normed_one, qkv_w, qkv_b, grad_att, tables, begins[:, None])
    grad_dense_own = dot_tn(attended, g_all)
    grad_qkv_w = dot_tn(normed_one, grad_z)
    grad_normed_one = dot_nt(grad_z, qkv_w)
    out_attn = dot(attended, dense_w)

    pre_act = dot(normed_two, up_w) + up_b
    act, slope = gelu_and_slope(pre_act)
    hidden = act.astype(BF16)
    grad_down_w = dot_tn(hidden, g_all)
    grad_pre = (dot_nt(g_all, down_w) * slope).astype(BF16)
    grad_up_w = dot_tn(normed_two, grad_pre)
    grad_normed_two = dot_nt(grad_pre, up_w)
    partial = out_attn + dot(hidden, down_w)

    mixed = (
        cube.scatter_sum(partial) + x_own.astype(F32) + dense_b + down_b
    ).astype(BF16)

    gy = cube.scatter_sum(grad_normed_one * gain_one + grad_normed_two * gain_two)
    x_here = x_own.astype(F32)
    mean_here = jnp.mean(x_here, axis=-1, keepdims=True)
    cent_here = x_here - mean_here
    scale_here = lax.rsqrt(jnp.mean(cent_here * cent_here, axis=-1, keepdims=True) + EPSILON)
    xhat_here = cent_here * scale_here
    dx = scale_here * (
        gy
        - jnp.mean(gy, axis=-1, keepdims=True)
        - xhat_here * jnp.mean(gy * xhat_here, axis=-1, keepdims=True)
    )
    grad_tokens = g_own.astype(F32) + dx

    vectors = jnp.stack(
        [
            jnp.sum(grad_normed_one * xhat, axis=0),
            jnp.sum(grad_normed_one, axis=0),
            jnp.sum(grad_normed_two * xhat, axis=0),
            jnp.sum(grad_normed_two, axis=0),
            jnp.sum(g_own.astype(F32), axis=0),
        ]
    )
    vectors = vectors.reshape(5, fsdp, shard).transpose(1, 0, 2).reshape(fsdp, 5 * shard)
    qkv_vec = jnp.zeros((seq, qkv_cols), F32)
    qkv_vec = lax.dynamic_update_slice_in_dim(
        qkv_vec, jnp.sum(grad_z.astype(F32), axis=0)[None], me, 0
    ).reshape(fsdp, -1)
    up_vec = jnp.zeros((fsdp, seq, unit), F32)
    up_vec = lax.dynamic_update_slice_in_dim(
        up_vec, jnp.sum(grad_pre.astype(F32), axis=0).reshape(fsdp, 1, unit), me, 1
    ).reshape(fsdp, seq * unit)
    vectors = jnp.concatenate([vectors, qkv_vec, up_vec], axis=1)

    def vector_for(index):
        return lax.dynamic_slice_in_dim(vectors, index, 1, 0)

    mine = vector_for(ring.me)
    for hop in range(1, fsdp):
        mine = mine + lax.ppermute(
            vector_for(lax.rem(ring.me + hop, fsdp)),
            "fsdp",
            [(i, (i + hop) % fsdp) for i in range(fsdp)],
        )
    mine = cube.total(mine)[0]
    small_grads = [mine[i * shard : (i + 1) * shard] for i in range(5)]
    qkv_b_grad = mine[5 * shard : 5 * shard + qkv_bias.shape[0]]
    up_b_grad = mine[5 * shard + qkv_bias.shape[0] :]

    def rows_of(whole, rows):
        return lambda index: lax.dynamic_slice_in_dim(whole, index * rows, rows, 0)

    down_part = ring.scatter_sum(rows_of(grad_down_w, unit), True).astype(BF16)
    up_part = ring.scatter_sum(rows_of(grad_up_w, shard), False).astype(BF16)
    qkv_part = ring.scatter_sum(rows_of(grad_qkv_w, shard), True).astype(BF16)

    dense_blocks = grad_dense_own.astype(BF16).reshape(spans, seq, dense_unit, width)
    pieces = cube.exchange(lambda other: lax.dynamic_slice_in_dim(dense_blocks, other, 1, 1)[:, 0])
    dense_cross = jnp.zeros((seq, spans, dense_unit, width), BF16)
    for mask, piece in pieces.items():
        dense_cross = lax.dynamic_update_slice_in_dim(dense_cross, piece[None], me ^ mask, 0)
    dense_cross = dense_cross.reshape(fsdp * dense_unit, width)
    dense_part = ring.scatter_sum(
        lambda index: rows_of(dense_cross, dense_unit)(index).astype(F32), False
    ).astype(BF16)

    def side_by_side(part, axis, shape):
        whole = jnp.zeros(shape, F32)
        for mask, piece in cube.gather(part).items():
            piece = jnp.expand_dims(piece.astype(F32).reshape(shape[:axis] + shape[axis + 1 :]), axis)
            whole = lax.dynamic_update_slice_in_dim(whole, piece, me ^ mask, axis)
        return whole

    down_grad = side_by_side(down_part, 0, (seq, unit, width)).reshape(down_weight.shape)
    up_grad = side_by_side(up_part, 2, (shard, fsdp, seq, unit)).reshape(up_weight.shape)
    qkv_grad = side_by_side(qkv_part, 1, (shard, seq, qkv_cols)).reshape(qkv_weight.shape)
    dense_grad = side_by_side(dense_part, 0, (seq, dense_unit, width)).reshape(dense_weight.shape)

    return (
        mixed[None],
        grad_tokens[None],
        small_grads[0],
        small_grads[1],
        small_grads[2],
        small_grads[3],
        qkv_grad,
        qkv_b_grad,
        dense_grad,
        small_grads[4],
        up_grad,
        up_b_grad,
        down_grad,
        small_grads[4],
    )


def solution(mesh):
    tokens = P("fsdp", "seq", None)
    vector, matrix = P("fsdp"), P("fsdp", None)
    return jax.shard_map(
        per_device,
        mesh=mesh,
        in_specs=(
            tokens, matrix, vector, vector, vector, vector, matrix, vector,
            matrix, vector, matrix, vector, matrix, vector, tokens,
        ),
        out_specs=(
            tokens, tokens, vector, vector, vector, vector, matrix, vector,
            matrix, vector, matrix, vector, matrix, vector,
        ),
        check_vma=False,
    )
```

```python
import functools

import jax
import jax.numpy as jnp
from jax import lax
from jax.experimental import pallas as pl
from jax.experimental.pallas import tpu as pltpu
from jax.sharding import PartitionSpec as P

HEAD_DIM = 64
ROT = 16
EPSILON = 1e-05
SCORE_SCALE = 0.125
MASKED_SCORE = -1e30
BF16 = jnp.bfloat16
F32 = jnp.float32
CONTRACT_ROWS = (((1,), (1,)), ((), ()))
CONTRACT_COLS = (((0,), (0,)), ((), ()))


def dot(a, b):
    return jnp.dot(a, b, preferred_element_type=F32)


def dot_nt(a, b):
    return lax.dot_general(a, b, CONTRACT_ROWS, preferred_element_type=F32)


def dot_tn(a, b):
    return lax.dot_general(a, b, CONTRACT_COLS, preferred_element_type=F32)


class Ring:
    def __init__(self, axis, size):
        self.axis, self.size = axis, size
        cycle = [i for i in range(0, size, 2)] + [i for i in range(size - 1, 0, -2)]
        self.up = [(cycle[i], cycle[(i + 1) % size]) for i in range(size)]
        self.down = [(b, a) for a, b in self.up]
        me = lax.axis_index(axis)
        self.me = me
        self.place = jnp.where(me % 2 == 0, me // 2, size - 1 - me // 2)

    def at(self, offset):
        place = lax.rem(self.place + (offset + self.size), self.size)
        half = self.size // 2
        return jnp.where(place < half, 2 * place, 2 * (self.size - 1 - place) + 1)

    def steps(self, longer_up):
        longer, shorter = self.size // 2, self.size - 1 - self.size // 2
        return (longer, shorter) if longer_up else (shorter, longer)

    def send_up(self, value):
        return lax.ppermute(value, self.axis, self.up)

    def send_down(self, value):
        return lax.ppermute(value, self.axis, self.down)

    def gather(self, chunk, longer_up):
        ups, downs = self.steps(longer_up)
        order, chunks = [self.me], [chunk]
        rising = falling = chunk
        for step in range(1, max(ups, downs) + 1):
            if step <= ups:
                rising = self.send_up(rising)
                order.append(self.at(-step))
                chunks.append(rising)
            if step <= downs:
                falling = self.send_down(falling)
                order.append(self.at(step))
                chunks.append(falling)
        return jnp.stack(order).astype(jnp.int32), chunks

    def scatter_sum(self, add, longer_up):
        ups, downs = self.steps(longer_up)
        rising, falling = (), ()
        for step in range(max(ups, downs), 0, -1):
            if step <= ups:
                rising = (self.send_up(add(self.at(step), *rising)),)
            if step <= downs:
                falling = (self.send_down(add(self.at(-step), *falling)),)
        return add(self.me, *rising, *falling)


def swap(value, mask, size):
    return lax.ppermute(value, "seq", [(i, i ^ mask) for i in range(size)])


def turn(values, cosine, sine_low, sine_high):
    width = values.shape[1]
    half = ROT // 2
    return (
        values * cosine
        + pltpu.roll(values, width - half, 1) * sine_low
        + pltpu.roll(values, half, 1) * sine_high
    )


def attention_body(
    heads, block_rows, window,
    normed, weight, bias, grad_out, cosine, sine_low, sine_high, first,
    out, grad_z,
    query_s, key_s, value_s, grad_s, grad_query, grad_key, grad_value, out_s,
):
    rows = normed.shape[0]
    pair = 2 * HEAD_DIM
    trio = 3 * HEAD_DIM
    chunk = block_rows

    def project(step, carry):
        here = pl.ds(pl.multiple_of(step * chunk, chunk), chunk)
        z = dot(normed[here, :], weight[...]) + bias[...]
        cos, low, high = cosine[here, :], sine_low[here, :], sine_high[here, :]
        for head in range(heads):
            base = head * trio
            turned = turn(z[:, base : base + pair], cos, low, high)
            query_s[head, here, :] = (turned[:, :HEAD_DIM].astype(BF16).astype(F32) * SCORE_SCALE).astype(BF16)
            key_s[head, here, :] = turned[:, HEAD_DIM:].astype(BF16)
            value_s[head, here, :] = z[:, base + pair : base + trio].astype(BF16)
            grad_s[head, here, :] = grad_out[here, head * HEAD_DIM : (head + 1) * HEAD_DIM]
        return carry

    lax.fori_loop(0, rows // chunk, project, 0)
    grad_key[...] = jnp.zeros_like(grad_key)
    grad_value[...] = jnp.zeros_like(grad_value)

    def one_block(head, q_here, k_here, q0, k0, span):
        q = query_s[head, q_here, :]
        do = grad_s[head, q_here, :]
        k = key_s[head, k_here, :]
        v = value_s[head, k_here, :]
        row = q0 + lax.broadcasted_iota(jnp.int32, (block_rows, span), 0)
        col = k0 + lax.broadcasted_iota(jnp.int32, (block_rows, span), 1)
        allowed = (col <= row) & (col >= first[q_here, :])
        scores = jnp.where(allowed, dot_nt(q, k), MASKED_SCORE)
        top = jnp.max(scores, axis=1, keepdims=True)
        weights = jnp.exp(scores - top)
        weights = weights / jnp.sum(weights, axis=1, keepdims=True)
        low = weights.astype(BF16)
        out_s[head, q_here, :] = dot(low, v).astype(BF16)
        grad_p = dot_nt(do, v)
        inner = jnp.sum(weights * grad_p, axis=1, keepdims=True)
        grad_sc = (weights * (grad_p - inner)).astype(BF16)
        grad_query[head, q_here, :] = dot(grad_sc, k) * SCORE_SCALE
        grad_key[head, k_here, :] += dot_tn(grad_sc, q)
        grad_value[head, k_here, :] += dot_tn(low, do)

    def one_head(head, carry):
        if rows // block_rows <= 8:
            for step in range(rows // block_rows):
                q0 = step * block_rows
                k0 = max(0, q0 - window)
                span = q0 + block_rows - k0
                one_block(head, pl.ds(q0, block_rows), pl.ds(k0, span), q0, k0, span)
        else:
            span = window + block_rows

            def at(step, inner):
                q0 = pl.multiple_of(step * block_rows, block_rows)
                k0 = pl.multiple_of(jnp.maximum(q0 - window, 0), block_rows)
                one_block(head, pl.ds(q0, block_rows), pl.ds(k0, span), q0, k0, span)
                return inner

            lax.fori_loop(0, rows // block_rows, at, 0)
        return carry

    lax.fori_loop(0, heads, one_head, 0)

    def finish(step, carry):
        here = pl.ds(pl.multiple_of(step * chunk, chunk), chunk)
        cos, low, high = cosine[here, :], sine_low[here, :], sine_high[here, :]
        for head in range(heads):
            base = head * trio
            both = jnp.concatenate([grad_query[head, here, :], grad_key[head, here, :]], axis=1)
            grad_z[here, base : base + pair] = turn(both, cos, -low, -high).astype(BF16)
            grad_z[here, base + pair : base + trio] = grad_value[head, here, :].astype(BF16)
            out[here, head * HEAD_DIM : (head + 1) * HEAD_DIM] = out_s[head, here, :]
        return carry

    lax.fori_loop(0, rows // chunk, finish, 0)


def attention(normed, weight, bias, grad_out, tables, first):
    rows = normed.shape[0]
    heads = weight.shape[1] // (3 * HEAD_DIM)
    block_rows = min(256, rows)
    window = rows // 2
    per_head = (heads, rows, HEAD_DIM)
    return pl.pallas_call(
        functools.partial(attention_body, heads, block_rows, window),
        out_shape=(
            jax.ShapeDtypeStruct((rows, heads * HEAD_DIM), BF16),
            jax.ShapeDtypeStruct((rows, heads * 3 * HEAD_DIM), BF16),
        ),
        scratch_shapes=[pltpu.VMEM(per_head, BF16) for _ in range(4)]
        + [pltpu.VMEM(per_head, F32) for _ in range(3)]
        + [pltpu.VMEM(per_head, BF16)],
        compiler_params=pltpu.CompilerParams(vmem_limit_bytes=56 * 1024 * 1024),
        name="attention",
    )(normed, weight, bias, grad_out, *tables, first)


def doc_layout(lengths, row_count):
    doc_ends = jnp.cumsum(lengths)
    doc_starts = doc_ends - lengths
    places = jnp.arange(row_count, dtype=jnp.int32)
    return jnp.max(
        jnp.where(doc_starts[None, :] <= places[:, None], doc_starts[None, :], 0), axis=1
    )


def rotary_tables(position):
    freqs = 1.0 / 10000.0 ** (jnp.arange(0, ROT, 2, dtype=F32) / ROT)
    angles = position.astype(F32)[:, None] * freqs[None, :]
    cos, sin = jnp.cos(angles), jnp.sin(angles)
    rows, half = position.shape[0], ROT // 2
    ones = jnp.ones((rows, HEAD_DIM - ROT), F32)
    zeros = jnp.zeros((rows, HEAD_DIM - ROT), F32)
    gap = jnp.zeros((rows, half), F32)
    cosine = jnp.concatenate([cos, cos, ones], axis=1)
    low = jnp.concatenate([-sin, gap, zeros], axis=1)
    high = jnp.concatenate([gap, sin, zeros], axis=1)
    return tuple(jnp.concatenate([t, t], axis=1) for t in (cosine, low, high))


def gelu_and_slope(values):
    upper = 0.5 * (1.0 + lax.erf(values * (0.5**0.5)))
    bell = jnp.exp(-0.5 * values * values) * 0.3989422804014327
    return values * upper, upper + values * bell


def plain_block(
    tokens, doc_lengths, ln1_gain, ln1_bias, ln2_gain, ln2_bias,
    qkv_weight, qkv_bias, dense_weight, dense_bias,
    up_weight, up_bias, down_weight, down_bias, cotangent,
):
    seq, fsdp = lax.axis_size("seq"), lax.axis_size("fsdp")
    me = lax.axis_index("seq")
    local_rows, width = tokens.shape[1], tokens.shape[2]
    row_count = local_rows * seq
    shard = width // fsdp
    hidden_all = up_weight.shape[1]
    unit = hidden_all // fsdp // seq
    qkv_cols = qkv_weight.shape[1] // seq
    dense_unit = shard // seq
    spans = fsdp // seq

    x_own, g_own = tokens[0], cotangent[0]

    small = jnp.concatenate(
        [ln1_gain, ln1_bias, ln2_gain, ln2_bias, dense_bias, down_bias, qkv_bias, up_bias]
    )[None]
    up_piece = lax.dynamic_slice_in_dim(
        up_weight.reshape(shard, fsdp, seq, unit), me, 1, 2
    ).reshape(shard, fsdp * unit)
    down_piece = lax.dynamic_slice_in_dim(down_weight, me * unit, unit, 0)
    qkv_piece = lax.dynamic_slice_in_dim(qkv_weight, me * qkv_cols, qkv_cols, 1)
    dense_piece = lax.dynamic_slice_in_dim(dense_weight, me * dense_unit, dense_unit, 0)

    def gather(value, axis):
        return lax.all_gather(value, axis, axis=0, tiled=True)

    x_all, g_all = gather(x_own, "seq"), gather(g_own, "seq")
    small_all = gather(small, "fsdp")
    dense_cross = gather(dense_piece, "fsdp")
    qkv_w, up_w, down_w = (gather(w, "fsdp") for w in (qkv_piece, up_piece, down_piece))

    def exchange(value):
        return lax.all_to_all(value, "seq", split_axis=0, concat_axis=0, tiled=True)

    dense_w = exchange(dense_cross).reshape(seq, spans, dense_unit, width)
    dense_w = dense_w.transpose(1, 0, 2, 3).reshape(spans * shard, width)

    def vector(index):
        return small_all[:, index * shard : (index + 1) * shard].reshape(width).astype(F32)

    gain_one, shift_one, gain_two, shift_two, dense_b, down_b = (vector(i) for i in range(6))
    base = 6 * shard
    qkv_b = small_all[:, base : base + qkv_bias.shape[0]].reshape(seq, qkv_cols)
    qkv_b = lax.dynamic_slice_in_dim(qkv_b, me, 1, 0).astype(F32)
    up_b = small_all[:, base + qkv_bias.shape[0] :].reshape(fsdp, seq, unit)
    up_b = lax.dynamic_slice_in_dim(up_b, me, 1, 1).reshape(1, fsdp * unit).astype(F32)

    begins = doc_layout(doc_lengths[0], row_count)
    tables = rotary_tables(jnp.arange(row_count, dtype=jnp.int32) - begins)

    xf = x_all.astype(F32)
    mean = jnp.mean(xf, axis=-1, keepdims=True)
    centered = xf - mean
    scale = lax.rsqrt(jnp.mean(centered * centered, axis=-1, keepdims=True) + EPSILON)
    xhat = centered * scale
    normed_one = (xhat * gain_one + shift_one).astype(BF16)
    normed_two = (xhat * gain_two + shift_two).astype(BF16)

    def seq_sum(value):
        value = lax.psum_scatter(value.astype(BF16), "seq", scatter_dimension=0, tiled=True)
        return value.astype(F32)

    def fsdp_sum(value):
        return lax.psum_scatter(value.astype(BF16), "fsdp", scatter_dimension=0, tiled=True)

    grad_att = dot_nt(g_all, dense_w).astype(BF16)
    attended, grad_z = attention(normed_one, qkv_w, qkv_b, grad_att, tables, begins[:, None])
    grad_dense_own = dot_tn(attended, g_all)
    grad_qkv_w = dot_tn(normed_one, grad_z)
    grad_normed_one = dot_nt(grad_z, qkv_w)
    out_attn = dot(attended, dense_w)

    pre_act = dot(normed_two, up_w) + up_b
    act, slope = gelu_and_slope(pre_act)
    hidden = act.astype(BF16)
    grad_down_w = dot_tn(hidden, g_all)
    grad_pre = (dot_nt(g_all, down_w) * slope).astype(BF16)
    grad_up_w = dot_tn(normed_two, grad_pre)
    grad_normed_two = dot_nt(grad_pre, up_w)
    partial = out_attn + dot(hidden, down_w)

    mixed = (
        seq_sum(partial) + x_own.astype(F32) + dense_b + down_b
    ).astype(BF16)

    gy = seq_sum(grad_normed_one * gain_one + grad_normed_two * gain_two)
    x_here = x_own.astype(F32)
    mean_here = jnp.mean(x_here, axis=-1, keepdims=True)
    cent_here = x_here - mean_here
    scale_here = lax.rsqrt(jnp.mean(cent_here * cent_here, axis=-1, keepdims=True) + EPSILON)
    xhat_here = cent_here * scale_here
    dx = scale_here * (
        gy
        - jnp.mean(gy, axis=-1, keepdims=True)
        - xhat_here * jnp.mean(gy * xhat_here, axis=-1, keepdims=True)
    )
    grad_tokens = g_own.astype(F32) + dx

    vectors = jnp.stack(
        [
            jnp.sum(grad_normed_one * xhat, axis=0),
            jnp.sum(grad_normed_one, axis=0),
            jnp.sum(grad_normed_two * xhat, axis=0),
            jnp.sum(grad_normed_two, axis=0),
            jnp.sum(g_own.astype(F32), axis=0),
        ]
    )
    vectors = vectors.reshape(5, fsdp, shard).transpose(1, 0, 2).reshape(fsdp, 5 * shard)
    qkv_vec = jnp.zeros((seq, qkv_cols), F32)
    qkv_vec = lax.dynamic_update_slice_in_dim(
        qkv_vec, jnp.sum(grad_z.astype(F32), axis=0)[None], me, 0
    ).reshape(fsdp, -1)
    up_vec = jnp.zeros((fsdp, seq, unit), F32)
    up_vec = lax.dynamic_update_slice_in_dim(
        up_vec, jnp.sum(grad_pre.astype(F32), axis=0).reshape(fsdp, 1, unit), me, 1
    ).reshape(fsdp, seq * unit)
    vectors = jnp.concatenate([vectors, qkv_vec, up_vec], axis=1)

    mine = lax.psum_scatter(vectors, "fsdp", scatter_dimension=0, tiled=True)
    mine = lax.psum(mine, "seq")[0]
    small_grads = [mine[i * shard : (i + 1) * shard] for i in range(5)]
    qkv_b_grad = mine[5 * shard : 5 * shard + qkv_bias.shape[0]]
    up_b_grad = mine[5 * shard + qkv_bias.shape[0] :]

    down_part, up_part, qkv_part = (fsdp_sum(w) for w in (grad_down_w, grad_up_w, grad_qkv_w))
    dense_blocks = grad_dense_own.astype(BF16).reshape(spans, seq, dense_unit, width)
    dense_blocks = exchange(dense_blocks.transpose(1, 0, 2, 3).reshape(-1, width))
    dense_part = fsdp_sum(dense_blocks)

    def side_by_side(part, shape, order):
        whole = gather(part[None], "seq").reshape((seq,) + shape).transpose(order)
        return whole.astype(F32)

    down_grad = side_by_side(down_part, (unit, width), (0, 1, 2)).reshape(down_weight.shape)
    up_grad = side_by_side(up_part, (shard, fsdp, unit), (1, 2, 0, 3)).reshape(up_weight.shape)
    qkv_grad = side_by_side(qkv_part, (shard, qkv_cols), (1, 0, 2)).reshape(qkv_weight.shape)
    dense_grad = side_by_side(dense_part, (dense_unit, width), (0, 1, 2)).reshape(
        dense_weight.shape
    )

    return (
        mixed[None],
        grad_tokens[None],
        small_grads[0],
        small_grads[1],
        small_grads[2],
        small_grads[3],
        qkv_grad,
        qkv_b_grad,
        dense_grad,
        small_grads[4],
        up_grad,
        up_b_grad,
        down_grad,
        small_grads[4],
    )


VMEM = pl.BlockSpec(memory_space=pltpu.VMEM)
SMEM = pl.BlockSpec(memory_space=pltpu.SMEM)
LANES = 128
PAD = 16
COLS = 256


def call(body, name, ins, outs, scratch=()):
    return pl.pallas_call(
        body,
        name=name,
        in_specs=[spec for spec, _ in ins],
        out_specs=[spec for spec, _, _ in outs],
        out_shape=[jax.ShapeDtypeStruct(shape, dtype) for _, shape, dtype in outs],
        scratch_shapes=list(scratch),
        compiler_params=pltpu.CompilerParams(vmem_limit_bytes=58 * 1024 * 1024),
    )(*[array for _, array in ins])


def rows_to_tile(rows, width):
    index = lax.broadcasted_iota(jnp.int32, (PAD, width), 0)
    tile = jnp.zeros((PAD, width), F32)
    for number, row in enumerate(rows):
        tile = jnp.where(index == number, row, tile)
    return tile


def pack_body(sizes, me, up, down, qkv, dense, *rest):
    seq, fsdp, shard, unit, qkv_cols, dense_unit = sizes
    vectors, (mlp, att) = rest[:8], rest[8:]
    width = fsdp * unit
    s = me[0]
    for block in range(qkv_cols // COLS):
        lane = pl.multiple_of(s * qkv_cols + block * COLS, LANES)
        att[block * shard : (block + 1) * shard, :] = qkv[:, pl.ds(lane, COLS)]
    base = qkv_cols // COLS * shard
    here = pl.ds(pl.multiple_of(s * dense_unit, PAD), dense_unit)
    for block in range(dense.shape[1] // COLS):
        at = base + block * dense_unit
        att[at : at + dense_unit, :] = dense[here, block * COLS : (block + 1) * COLS]
    for block in range(fsdp):
        lane = pl.multiple_of(block * seq * unit + s * unit, LANES)
        mlp[:shard, block * unit : (block + 1) * unit] = up[:, pl.ds(lane, unit)]
    mlp[shard : shard + unit, :] = down[pl.ds(pl.multiple_of(s * unit, unit), unit), :]
    values = [v[...].astype(F32) for v in vectors]
    first, second = jnp.concatenate(values[:6], axis=1), jnp.concatenate(values[6:], axis=1)
    first, second = (
        jnp.concatenate([v, jnp.zeros((1, width - v.shape[1]), F32)], axis=1)
        for v in (first, second)
    )
    mlp[shard + unit :, :] = rows_to_tile([first, second], width).astype(BF16)


def mlp_body(
    sizes, order, me, xhat, grad, *rest
):
    seq, fsdp, shard, unit, qkv_cols, dense_unit = sizes
    chunks, rest = rest[:fsdp], rest[fsdp:]
    normed_one, hidden, grad_pre, up, down, grads, vectors, qkv_b, up_sum = rest[:9]
    normed_two, qkv_all, up_b, row = rest[9:]
    s = me[0]
    qkv_shard = seq * qkv_cols // fsdp
    for number, chunk in enumerate(chunks):
        f = order[number]
        up[pl.ds(pl.multiple_of(f * shard, shard), shard), :] = chunk[:shard, :]
        down[pl.ds(pl.multiple_of(f * unit, unit), unit), :] = chunk[shard : shard + unit, :]
        small = chunk[shard + unit :, :].astype(F32)
        here = pl.ds(pl.multiple_of(f * shard, shard), shard)
        for v in range(6):
            vectors[v : v + 1, here] = small[0:1, v * shard : (v + 1) * shard]
        qkv_all[:, pl.ds(pl.multiple_of(f * qkv_shard, LANES), qkv_shard)] = small[1:2, :qkv_shard]
        row[...] = small[1:2, qkv_shard : qkv_shard + seq * unit]
        up_b[:, pl.ds(pl.multiple_of(f * unit, unit), unit)] = row[
            :, pl.ds(pl.multiple_of(s * unit, unit), unit)
        ]
    qkv_b[...] = qkv_all[:, pl.ds(pl.multiple_of(s * qkv_cols, LANES), qkv_cols)]

    rows = xhat.shape[0]
    block = 256
    up_sum[...] = jnp.zeros_like(up_sum)

    def forward(step, carry):
        here = pl.ds(pl.multiple_of(step * block, block), block)
        values = xhat[here, :]
        normed_one[here, :] = (values * vectors[0:1, :] + vectors[1:2, :]).astype(BF16)
        two = (values * vectors[2:3, :] + vectors[3:4, :]).astype(BF16)
        normed_two[here, :] = two
        act, slope = gelu_and_slope(dot(two, up[...]) + up_b[...])
        hidden[here, :] = act.astype(BF16)
        pre = (dot_nt(grad[here, :], down[...]) * slope).astype(BF16)
        grad_pre[here, :] = pre
        up_sum[...] += jnp.sum(pre.astype(F32), axis=0, keepdims=True)
        return carry

    lax.fori_loop(0, rows // block, forward, 0)
    for two in range(fsdp // 2):
        part = dot_tn(normed_two[:, two * 2 * shard : (two + 1) * 2 * shard], grad_pre[...])
        grads[2 * two, :shard, :] = part[:shard].astype(BF16)
        grads[2 * two + 1, :shard, :] = part[shard:].astype(BF16)
        part = dot_tn(hidden[:, two * 2 * unit : (two + 1) * 2 * unit], grad[...])
        grads[2 * two, shard:, :] = part[:unit].astype(BF16)
        grads[2 * two + 1, shard:, :] = part[unit:].astype(BF16)


def unpack_body(sizes, order, *rest):
    seq, fsdp, shard, unit, qkv_cols, dense_unit = sizes
    chunks, (qkv_w, dense) = rest[:fsdp], rest[fsdp:]
    base = qkv_cols // COLS * shard
    for number, chunk in enumerate(chunks):
        f = order[number]
        here = pl.ds(pl.multiple_of(f * shard, shard), shard)
        for block in range(qkv_cols // COLS):
            qkv_w[here, block * COLS : (block + 1) * COLS] = chunk[block * shard : (block + 1) * shard, :]
        dense[f, :, :] = chunk[base:, :]


def grad_out_body(sizes, grad, dense, dense_w, grad_att):
    seq, fsdp, shard, unit, qkv_cols, dense_unit = sizes
    spans = fsdp // seq
    for source in range(seq):
        for span in range(spans):
            row = span * shard + source * dense_unit
            for block in range(dense_w.shape[1] // COLS):
                dense_w[row : row + dense_unit, block * COLS : (block + 1) * COLS] = dense[
                    source * spans + span, block * dense_unit : (block + 1) * dense_unit, :
                ]
    grad_att[...] = dot_nt(grad[...], dense_w[...]).astype(BF16)


def attention_part(normed, weight, bias, grad_out, tables, first, part, parts):
    rows = normed.shape[0]
    heads = weight.shape[1] // (3 * HEAD_DIM) // parts
    per_head = (heads, rows, HEAD_DIM)

    def columns(array, heads_width):
        return pl.BlockSpec(
            (array.shape[0], heads * heads_width),
            lambda i: (0, part),
            pipeline_mode=pl.Buffered(1),
        )

    def whole(array):
        return pl.BlockSpec(array.shape, lambda i: (0, 0), pipeline_mode=pl.Buffered(1))

    ins = [normed, weight, bias, grad_out, *tables, first]
    specs = [whole(a) for a in ins]
    specs[1], specs[2] = columns(weight, 3 * HEAD_DIM), columns(bias, 3 * HEAD_DIM)
    specs[3] = columns(grad_out, HEAD_DIM)
    shapes = ((rows, heads * HEAD_DIM), (rows, heads * 3 * HEAD_DIM))
    return pl.pallas_call(
        functools.partial(attention_body, heads, min(256, rows), rows // 2),
        grid=(1,),
        in_specs=specs,
        out_specs=[pl.BlockSpec(s, lambda i: (0, 0), pipeline_mode=pl.Buffered(1)) for s in shapes],
        out_shape=[jax.ShapeDtypeStruct(s, BF16) for s in shapes],
        scratch_shapes=[pltpu.VMEM(per_head, BF16) for _ in range(4)]
        + [pltpu.VMEM(per_head, F32) for _ in range(3)]
        + [pltpu.VMEM(per_head, BF16)],
        compiler_params=pltpu.CompilerParams(vmem_limit_bytes=48 * 1024 * 1024),
        name=f"attention_{part}",
    )(*ins)


def qkv_grads_body(
    sizes, parts, me, *rest
):
    seq, fsdp, shard, unit, qkv_cols, dense_unit = sizes
    outs, grad_zs = rest[:parts], rest[parts : 2 * parts]
    normed, grad, qkv_w, grad_pre, up, xhat, vectors, up_sum = rest[2 * parts : 2 * parts + 8]
    grads, grad_dense, gy_send, gy_keep = rest[2 * parts + 8 : 2 * parts + 12]
    grad_z, sums, qkv_sum, up_row = rest[2 * parts + 12 :]
    s = me[0]
    spans = fsdp // seq
    rows, width = xhat.shape
    local = rows // seq
    part_cols = qkv_cols // parts
    base = qkv_cols // COLS * shard
    for part in range(parts):
        grad_z[:, part * part_cols : (part + 1) * part_cols] = grad_zs[part][...]
    for two in range(fsdp // 2):
        part = dot_tn(normed[:, two * 2 * shard : (two + 1) * 2 * shard], grad_z[...]).astype(BF16)
        for block in range(qkv_cols // COLS):
            cols = slice(block * COLS, (block + 1) * COLS)
            grads[2 * two, block * shard : (block + 1) * shard, :] = part[:shard, cols]
            grads[2 * two + 1, block * shard : (block + 1) * shard, :] = part[shard:, cols]
    heads_part = outs[0].shape[1]
    for part in range(parts):
        piece = dot_tn(outs[part][...], grad[...]).astype(BF16)
        for at in range(0, heads_part, dense_unit):
            row = part * heads_part + at
            span, target = row // shard, row % shard // dense_unit
            for block in range(width // COLS):
                grad_dense[
                    target * spans + span, block * dense_unit : (block + 1) * dense_unit, :
                ] = piece[at : at + dense_unit, block * COLS : (block + 1) * COLS]
    sums[...] = jnp.zeros_like(sums)

    def block_of(index):
        here = pl.ds(pl.multiple_of(index * local, local), local)
        one = dot_nt(grad_z[here, :], qkv_w[...])
        two = dot_nt(grad_pre[here, :], up[...])
        values = xhat[here, :]
        sums[0:1, :] += jnp.sum(one * values, axis=0, keepdims=True)
        sums[1:2, :] += jnp.sum(one, axis=0, keepdims=True)
        sums[2:3, :] += jnp.sum(two * values, axis=0, keepdims=True)
        sums[3:4, :] += jnp.sum(two, axis=0, keepdims=True)
        return one * vectors[0:1, :] + two * vectors[2:3, :]

    half = seq // 2
    for number in range(half):
        gy_send[number] = block_of((s ^ 1) ^ (2 * number)).astype(BF16)
        gy_keep[number] = block_of(s ^ (2 * number)).astype(BF16)
    own = grad[pl.ds(pl.multiple_of(s * local, local), local), :].astype(F32)
    sums[4:5, :] = jnp.sum(own, axis=0, keepdims=True)
    qkv_sum[...] = jnp.zeros_like(qkv_sum)
    qkv_sum[:, pl.ds(pl.multiple_of(s * qkv_cols, LANES), qkv_cols)] = jnp.sum(
        grad_z[...].astype(F32), axis=0, keepdims=True
    )
    up_row[...] = jnp.zeros_like(up_row)
    qkv_shard = seq * qkv_cols // fsdp
    for f in range(fsdp):
        up_row[:, pl.ds(pl.multiple_of(s * unit, unit), unit)] = up_sum[:, f * unit : (f + 1) * unit]
        flat = [sums[v : v + 1, f * shard : (f + 1) * shard] for v in range(5)]
        flat.append(qkv_sum[:, f * qkv_shard : (f + 1) * qkv_shard])
        flat.append(up_row[...])
        flat = jnp.concatenate(flat, axis=1)
        lines = [flat[:, at : at + COLS] for at in range(0, flat.shape[1], COLS)]
        grads[f, base:, :] = rows_to_tile(lines, COLS).astype(BF16)


def outputs_body(sizes, parts, me, *rest):
    seq, fsdp, shard, unit, qkv_cols, dense_unit = sizes
    outs, (hidden, down, dense_w, send, keep) = rest[:parts], rest[parts:]
    s = me[0]
    local = hidden.shape[0] // seq

    def block_of(index):
        here = pl.ds(pl.multiple_of(index * local, local), local)
        total = dot(hidden[here, :], down[...])
        for part in range(parts):
            heads_part = outs[part].shape[1]
            total += dot(outs[part][here, :], dense_w[part * heads_part : (part + 1) * heads_part, :])
        return total

    for number in range(seq // 2):
        send[number] = block_of((s ^ 1) ^ (2 * number)).astype(BF16)
        keep[number] = block_of(s ^ (2 * number)).astype(BF16)


def ring_add(index, received, pieces, name):
    rows = [p.shape[1] for p in pieces]
    width = pieces[0].shape[2]

    def body(where, *refs):
        out = refs[-1]
        at = 0
        for piece, count in zip(refs, rows):
            total = piece[0].astype(F32)
            for item in refs[len(rows) : -1]:
                total += item[at : at + count, :].astype(F32)
            out[at : at + count, :] = total.astype(BF16)
            at += count

    total = sum(rows)
    return pl.pallas_call(
        body,
        name=name,
        grid_spec=pltpu.PrefetchScalarGridSpec(
            num_scalar_prefetch=1,
            grid=(1,),
            in_specs=[pl.BlockSpec((1, r, width), lambda i, where: (where[0], 0, 0)) for r in rows]
            + [pl.BlockSpec((total, width), lambda i, where: (0, 0)) for _ in received],
            out_specs=pl.BlockSpec((total, width), lambda i, where: (0, 0)),
        ),
        out_shape=jax.ShapeDtypeStruct((total, width), BF16),
    )(index.astype(jnp.int32).reshape(1), *pieces, *received)


def mlp_out_body(sizes, me, *rest):
    seq, fsdp, shard, unit, qkv_cols, dense_unit = sizes
    parts, (up, down) = rest[:seq], rest[seq:]
    for mask, part in enumerate(parts):
        source = me[0] ^ mask
        for f in range(fsdp):
            lane = pl.multiple_of(f * seq * unit + source * unit, LANES)
            up[:, pl.ds(lane, unit)] = part[:shard, f * unit : (f + 1) * unit].astype(F32)
        down[pl.ds(pl.multiple_of(source * unit, unit), unit), :] = part[shard:, :].astype(F32)


def att_out_body(sizes, me, *rest):
    seq, fsdp, shard, unit, qkv_cols, dense_unit = sizes
    parts, (qkv, dense, *small) = rest[:seq], rest[seq:]
    base = qkv_cols // COLS * shard
    lines = jnp.zeros((PAD, COLS), F32)
    for mask, part in enumerate(parts):
        source = me[0] ^ mask
        for block in range(qkv_cols // COLS):
            lane = pl.multiple_of(source * qkv_cols + block * COLS, LANES)
            qkv[:, pl.ds(lane, COLS)] = part[block * shard : (block + 1) * shard, :].astype(F32)
        here = pl.ds(pl.multiple_of(source * dense_unit, PAD), dense_unit)
        for block in range(dense.shape[1] // COLS):
            at = base + PAD + block * dense_unit
            dense[here, block * COLS : (block + 1) * COLS] = part[at : at + dense_unit, :].astype(F32)
        lines += part[base : base + PAD, :].astype(F32)
    count = sum(v.shape[1] for v in small)
    flat = jnp.concatenate([lines[r : r + 1, :] for r in range(count // COLS)], axis=1)
    at = 0
    for out in small:
        out[...] = flat[:, at : at + out.shape[1]]
        at += out.shape[1]


def fast_block(
    tokens, doc_lengths, ln1_gain, ln1_bias, ln2_gain, ln2_bias,
    qkv_weight, qkv_bias, dense_weight, dense_bias,
    up_weight, up_bias, down_weight, down_bias, cotangent,
):
    seq, fsdp = lax.axis_size("seq"), lax.axis_size("fsdp")
    ring = Ring("fsdp", fsdp)
    me = lax.axis_index("seq")
    s = me.astype(jnp.int32).reshape(1)
    local_rows, width = tokens.shape[1], tokens.shape[2]
    row_count = local_rows * seq
    shard = width // fsdp
    unit = up_weight.shape[1] // fsdp // seq
    qkv_cols = qkv_weight.shape[1] // seq
    dense_unit = shard // seq
    sizes = (seq, fsdp, shard, unit, qkv_cols, dense_unit)
    mlp_rows = shard + unit
    att_rows = qkv_cols // COLS * shard + width // COLS * dense_unit
    hidden_units = fsdp * unit
    parts = 2
    x_own, g_own = tokens[0], cotangent[0]

    def spec(body):
        return functools.partial(body, sizes)

    small = [ln1_gain, ln1_bias, ln2_gain, ln2_bias, dense_bias, down_bias, qkv_bias, up_bias]
    mlp_own, att_own = call(
        spec(pack_body), "pack",
        [(SMEM, s)]
        + [(VMEM, w) for w in (up_weight, down_weight, qkv_weight, dense_weight)]
        + [(VMEM, v.reshape(1, -1)) for v in small],
        [(VMEM, (mlp_rows + PAD, width), BF16), (VMEM, (att_rows, COLS), BF16)],
    )

    mlp_order, mlp_chunks = ring.gather(mlp_own, True)

    def gather_rows(value):
        found = {0: value}
        found[2] = swap(value, 2, seq)
        found[1] = swap(value, 1, seq)
        found[3] = swap(found[2], 1, seq)
        whole = jnp.zeros((row_count, width), BF16)
        for mask, piece in found.items():
            whole = lax.dynamic_update_slice_in_dim(whole, piece, (me ^ mask) * local_rows, 0)
        return whole

    x_all = gather_rows(x_own)
    g_all = gather_rows(g_own)
    att_order, att_chunks = ring.gather(att_own, False)

    begins = doc_layout(doc_lengths[0], row_count)
    tables = rotary_tables(jnp.arange(row_count, dtype=jnp.int32) - begins)

    def norm(values):
        values = values.astype(F32)
        centered = values - jnp.mean(values, axis=-1, keepdims=True)
        scale = lax.rsqrt(jnp.mean(centered * centered, axis=-1, keepdims=True) + EPSILON)
        return centered * scale, scale

    xhat, _ = norm(x_all)

    normed_one, hidden, grad_pre, up_w, down_w, mlp_grads, vectors, qkv_b, up_sum = call(
        spec(mlp_body), "mlp",
        [(SMEM, mlp_order), (SMEM, s), (VMEM, xhat), (VMEM, g_all)]
        + [(VMEM, c) for c in mlp_chunks],
        [
            (VMEM, (row_count, width), BF16),
            (VMEM, (row_count, hidden_units), BF16),
            (VMEM, (row_count, hidden_units), BF16),
            (VMEM, (width, hidden_units), BF16),
            (VMEM, (hidden_units, width), BF16),
            (VMEM, (fsdp, mlp_rows, width), BF16),
            (VMEM, (8, width), F32),
            (VMEM, (1, qkv_cols), F32),
            (VMEM, (1, hidden_units), F32),
        ],
        [
            pltpu.VMEM((row_count, width), BF16),
            pltpu.VMEM((1, seq * qkv_cols), F32),
            pltpu.VMEM((1, hidden_units), F32),
            pltpu.VMEM((1, seq * unit), F32),
        ],
    )

    qkv_w, dense_cross = call(
        spec(unpack_body), "unpack",
        [(SMEM, att_order)] + [(VMEM, c) for c in att_chunks],
        [(VMEM, (width, qkv_cols), BF16), (VMEM, (fsdp, width // COLS * dense_unit, COLS), BF16)],
    )

    def exchange(value):
        return lax.all_to_all(value, "seq", split_axis=0, concat_axis=0, tiled=True)

    dense_w, grad_att = call(
        spec(grad_out_body), "grad_out",
        [(VMEM, g_all), (VMEM, exchange(dense_cross))],
        [(VMEM, (fsdp // seq * shard, width), BF16), (VMEM, (row_count, fsdp // seq * shard), BF16)],
    )
    pairs = [
        attention_part(normed_one, qkv_w, qkv_b, grad_att, tables, begins[:, None], part, parts)
        for part in range(parts)
    ]
    attended, grad_zs = [p[0] for p in pairs], [p[1] for p in pairs]

    half = (seq // 2, local_rows, width)
    att_grads, grad_dense, gy_send, gy_keep = call(
        functools.partial(qkv_grads_body, sizes, parts), "qkv_grads",
        [(SMEM, s)]
        + [(VMEM, a) for a in attended]
        + [(VMEM, z) for z in grad_zs]
        + [(VMEM, a) for a in (normed_one, g_all, qkv_w, grad_pre, up_w, xhat, vectors, up_sum)],
        [
            (VMEM, (fsdp, qkv_cols // COLS * shard + PAD, COLS), BF16),
            (VMEM, (fsdp, width // COLS * dense_unit, COLS), BF16),
            (VMEM, half, BF16),
            (VMEM, half, BF16),
        ],
        [
            pltpu.VMEM((row_count, qkv_cols), BF16),
            pltpu.VMEM((8, width), F32),
            pltpu.VMEM((1, seq * qkv_cols), F32),
            pltpu.VMEM((1, seq * unit), F32),
        ],
    )
    grad_dense = exchange(grad_dense)
    out_send, out_keep = call(
        functools.partial(outputs_body, sizes, parts), "outputs",
        [(SMEM, s)] + [(VMEM, a) for a in (*attended, hidden, down_w, dense_w)],
        [(VMEM, half, BF16), (VMEM, half, BF16)],
    )

    def seq_sum(send, keep):
        both = keep.astype(F32) + swap(send, 1, seq).astype(F32)
        return both[0] + swap(both[1].astype(BF16), 2, seq).astype(F32)

    mlp_part = ring.scatter_sum(
        lambda index, *got: ring_add(index, got, [mlp_grads], "add_mlp"), True
    )
    att_part = ring.scatter_sum(
        lambda index, *got: ring_add(index, got, [att_grads, grad_dense], "add_att"), False
    )

    mixed = (
        seq_sum(out_send, out_keep) + x_own.astype(F32) + vectors[4] + vectors[5]
    ).astype(BF16)
    gy = seq_sum(gy_send, gy_keep)
    xhat_here, scale_here = norm(x_own)
    dx = scale_here * (
        gy
        - jnp.mean(gy, axis=-1, keepdims=True)
        - xhat_here * jnp.mean(gy * xhat_here, axis=-1, keepdims=True)
    )
    grad_tokens = g_own.astype(F32) + dx

    def all_parts(value):
        across = swap(value, 2, seq)
        return [value, swap(value, 1, seq), across, swap(across, 1, seq)]

    up_grad, down_grad = call(
        spec(mlp_out_body), "mlp_out",
        [(SMEM, s)] + [(VMEM, p) for p in all_parts(mlp_part)],
        [(VMEM, up_weight.shape, F32), (VMEM, down_weight.shape, F32)],
    )
    qkv_grad, dense_grad, *small_grads = call(
        spec(att_out_body), "att_out",
        [(SMEM, s)] + [(VMEM, p) for p in all_parts(att_part)],
        [(VMEM, qkv_weight.shape, F32), (VMEM, dense_weight.shape, F32)]
        + [(VMEM, (1, shard), F32)] * 5
        + [(VMEM, (1, qkv_bias.shape[0]), F32), (VMEM, (1, up_bias.shape[0]), F32)],
    )
    small_grads = [v[0] for v in small_grads]
    return (
        mixed[None],
        grad_tokens[None],
        small_grads[0],
        small_grads[1],
        small_grads[2],
        small_grads[3],
        qkv_grad,
        small_grads[5],
        dense_grad,
        small_grads[4],
        up_grad,
        small_grads[6],
        down_grad,
        small_grads[4],
    )


def per_device(*args):
    tokens, qkv_weight, up_weight = args[0], args[6], args[10]
    seq, fsdp = lax.axis_size("seq"), lax.axis_size("fsdp")
    shard = tokens.shape[2] // fsdp
    unit = up_weight.shape[1] // fsdp // seq
    fits = (
        seq == 4
        and fsdp % seq == 0
        and tokens.shape[1] * seq <= 1024
        and shard % LANES == 0
        and unit % LANES == 0
        and qkv_weight.shape[1] // seq % (2 * COLS) in (0, COLS)
        and (shard // seq) % PAD == 0
    )
    return (fast_block if fits else plain_block)(*args)


def solution(mesh):
    tokens = P("fsdp", "seq", None)
    vector, matrix = P("fsdp"), P("fsdp", None)
    return jax.shard_map(
        per_device,
        mesh=mesh,
        in_specs=(
            tokens, matrix, vector, vector, vector, vector, matrix, vector,
            matrix, vector, matrix, vector, matrix, vector, tokens,
        ),
        out_specs=(
            tokens, tokens, vector, vector, vector, vector, matrix, vector,
            matrix, vector, matrix, vector, matrix, vector,
        ),
        check_vma=False,
    )
```
